256 devices in a mesh: slab: 128 (over z, y_lo, x, core), plane: 2 (over y_hi).
Axes of the slice: x: 4, y: 4 (y_hi: 2, y_lo: 2; y = y_hi * 2 + y_lo), z: 8, core: 2. Of those that a mesh axis runs over, the one named last changes fastest.
Arguments:
- probe_pos: bfloat16 [3, 32768], P(None, ('slab', 'plane')), may hold values from 0 to 2
- atom_pos: bfloat16 [3, 32768], P(None, ('slab', 'plane')), may hold values from 0 to 2
- atom_feat: bfloat16 [128, 32768], P(None, ('slab', 'plane')), may hold values from -6 to 6
- neighbours: int32 [32, 32768], P(None, ('slab', 'plane')), may hold values from 0 to 32767, as said below
- valid: int32 [32, 32768], P(None, ('slab', 'plane')), may hold values 0 or 1
- w_radial1: float32 [64, 8], replicated, may hold values from -2 to 2
- w_radial2: bfloat16 [640, 64], replicated, may hold values from -0.75 to 0.75
- readout: float32 [5, 128], replicated, may hold values from -0.5 to 0.5
- cotangent: float32 [32768], P(('slab', 'plane')), may hold values from -6 to 6
Outputs:
- density: float32 [32768], P(('slab', 'plane'))
- grad_feat: float32 [128, 32768], P(None, ('slab', 'plane'))
- grad_radial1: float32 [64, 8], replicated
- grad_radial2: float32 [640, 64], replicated
- grad_readout: float32 [5, 128], replicated
The draws below stay inside these ranges and needn't reach their ends.
Inputs may be any that keep to these rules, and one draw needn't show every extreme that they name: `neighbours`: the atom of every slot of probe p lies in the slab of p (atoms a with a // 256 = p // 256) or in one of the two slabs beside it on the periodic cycle of slabs.
All inputs are finite; a program needn't handle non-finite values. No bound on the sum of `valid` on one device may be relied on, other than what follows from the above.
Results may differ from the reference program's by a relative error of at most 0.0049.
Values may be sent and summed in bfloat16 or wider, within the bound.
No kernel may reach another device: no remote copies, remote signals or barrier semaphores. Data moves between devices by JAX's collectives and lax.ppermute only.
A program may use at most 128 MiB of HBM per device.

```python
import math
import jax
import jax.numpy as jnp
from jax import lax

C = 128
DEG = 5
NB = 8
RH = 64
NBR = 32
PROBE_DEV = 128
ATOM_SLAB = 256
ATOMS = 32768
PROBE_SLAB = 256
PROBES = 32768
N_SLAB = 128


def draw_neighbours(key, part):
    key_offset, key_local = jax.random.split(key)
    offset = jax.random.randint(key_offset, (NBR, PROBES), -1, 2)
    local_row = jax.random.randint(key_local, (NBR, PROBES), 0, ATOM_SLAB)
    slab_of = jnp.arange(PROBES, dtype=jnp.int32) // PROBE_SLAB
    return ((slab_of[None, :] + offset) % N_SLAB * ATOM_SLAB + local_row).astype(jnp.int32)


def plant(drawn, rng, least, top_value):
    index_at = [jax.random.randint(jax.random.fold_in(rng, axis), (), 0, length) for axis, length in enumerate(drawn.shape)]
    longest = drawn.shape.index(max(drawn.shape))
    neighbour = index_at[:longest] + [(index_at[longest] + 1) % drawn.shape[longest]] + index_at[longest + 1:]
    return drawn.at[tuple(index_at)].set(least).at[tuple(neighbour)].set(top_value)


def block_scale(own_key, dims, cuts, low, top_value):
    def one(position, blocks):
        steps = jax.random.uniform(jax.random.fold_in(jax.random.fold_in(own_key, 6), position), (blocks,), jnp.float32, low / len(cuts), top_value / len(cuts))
        return jnp.repeat(jnp.exp(steps), dims[position] // blocks).reshape((-1,) + (1,) * (len(dims) - position - 1))

    level = one(*cuts[0])
    for cut in cuts[1:]:
        level = level * one(*cut)
    return level


def bell_draw(own_key, dims, spread, reach, shards=(), kind=jnp.bfloat16):
    drawn = jax.random.normal(own_key, dims, jnp.float32) * spread
    if len(shards) > 0:
        drawn = block_scale(own_key, dims, shards, -0.22, 0.18) * drawn
    return jnp.clip(drawn, min=-reach, max=reach).astype(kind)


def setup_inputs(seed: int = 0) -> dict:
    streams_of = jax.random.split(jax.random.key(seed), 10)
    probe_pos = jnp.clip(2.0 * jax.random.uniform(streams_of[0], (3, PROBES), jnp.float32) ** block_scale(streams_of[0], (3, PROBES), ((1, 256),), -0.2, 0.2), 0.0, 2.0).astype(jnp.bfloat16)
    atom_pos = jnp.clip(2.0 * jax.random.uniform(streams_of[1], (3, ATOMS), jnp.float32) ** block_scale(streams_of[1], (3, ATOMS), ((1, 256),), -0.2, 0.2), 0.0, 2.0).astype(jnp.bfloat16)
    atom_feat = bell_draw(streams_of[2], (C, ATOMS), 1.0, 6.0, ((1, 256),))
    neighbours = draw_neighbours(jax.random.fold_in(streams_of[9], 71), 0)
    valid = plant((jax.random.randint(streams_of[4], (NBR, PROBES), 0, 4) < 3).astype(jnp.int32), jax.random.fold_in(streams_of[4], 1), 0, 1)
    w_radial1 = bell_draw(streams_of[5], (RH, NB), NB ** -0.5, 2.0, (), jnp.float32)
    w_radial2 = bell_draw(streams_of[6], (DEG * C, RH), RH ** -0.5, 0.75)
    readout = bell_draw(streams_of[7], (DEG, C), C ** -0.5, 0.5, (), jnp.float32)
    cotangent = bell_draw(streams_of[8], (PROBES,), 1.0, 6.0, ((0, 256),), jnp.float32)
    return {"probe_pos": probe_pos, "atom_pos": atom_pos, "atom_feat": atom_feat, "neighbours": neighbours, "valid": valid, "w_radial1": w_radial1, "w_radial2": w_radial2, "readout": readout, "cotangent": cotangent}


slab_width = 2.0
soften = 0.25

def harmonics(along_x, along_y, along_z):
    sq_x = along_x * along_x
    sq_y = along_y * along_y
    sq_z = along_z * along_z
    root3 = math.sqrt(3.0)
    root15 = math.sqrt(15.0)
    root5 = math.sqrt(5.0)
    coef_a1 = math.sqrt(35.0 / 8.0)
    coef_a2 = math.sqrt(105.0)
    coef_a3 = math.sqrt(21.0 / 8.0)
    coef_a4 = math.sqrt(7.0) / 2.0
    coef_b1 = 3.0 * math.sqrt(35.0) / 2.0
    coef_b2 = 3.0 * math.sqrt(70.0) / 4.0
    coef_b3 = 3.0 * math.sqrt(5.0) / 2.0
    coef_b4 = 3.0 * math.sqrt(10.0) / 4.0
    rows_out = [jnp.ones_like(along_x), root3 * along_y, root3 * along_z, root3 * along_x, root15 * along_x * along_y, root15 * along_y * along_z, root5 / 2.0 * (3.0 * sq_z - 1.0), root15 * along_x * along_z, root15 / 2.0 * (sq_x - sq_y), coef_a1 * along_y * (3.0 * sq_x - sq_y), coef_a2 * along_x * along_y * along_z, coef_a3 * along_y * (5.0 * sq_z - 1.0), coef_a4 * along_z * (5.0 * sq_z - 3.0), coef_a3 * along_x * (5.0 * sq_z - 1.0), coef_a2 / 2.0 * along_z * (sq_x - sq_y), coef_a1 * along_x * (sq_x - 3.0 * sq_y), coef_b1 * along_x * along_y * (sq_x - sq_y), coef_b2 * along_y * along_z * (3.0 * sq_x - sq_y), coef_b3 * along_x * along_y * (7.0 * sq_z - 1.0), coef_b4 * along_y * along_z * (7.0 * sq_z - 3.0), 0.375 * (35.0 * sq_z * sq_z - 30.0 * sq_z + 3.0), coef_b4 * along_x * along_z * (7.0 * sq_z - 3.0), coef_b3 / 2.0 * (sq_x - sq_y) * (7.0 * sq_z - 1.0), coef_b2 * along_x * along_z * (sq_x - 3.0 * sq_y), coef_b1 / 4.0 * (sq_x * (sq_x - 3.0 * sq_y) - sq_y * (3.0 * sq_x - sq_y))]
    return jnp.stack(rows_out)

def probe_block(features, atom_xyz, probe_xyz, offset, weight_mask, cot_block, w_radial1, w_radial2, readout):
    slots, block_len = weight_mask.shape
    edge_count = slots * block_len
    channels = features.shape[0]
    degrees = readout.shape[0]
    probe_tile = jnp.broadcast_to(probe_xyz[:, None, :], (3, slots, block_len)).reshape(3, edge_count)
    delta_x = atom_xyz[0] - probe_tile[0]
    delta_y = atom_xyz[1] - probe_tile[1]
    delta_z = atom_xyz[2] + slab_width * offset.reshape(edge_count) - probe_tile[2]
    radius = jnp.sqrt(delta_x * delta_x + delta_y * delta_y + delta_z * delta_z + soften)
    sphere = harmonics(delta_x / radius, delta_y / radius, delta_z / radius)
    centres = 0.75 * jnp.arange(w_radial1.shape[1], dtype=jnp.float32)
    radial_basis = jnp.exp(-2.0 * (radius[None, :] - centres[:, None]) ** 2)
    preact = jnp.dot(w_radial1, radial_basis, precision=lax.Precision.HIGHEST)
    hidden = jax.nn.silu(preact).astype(jnp.bfloat16)
    radial = jnp.dot(w_radial2, hidden, preferred_element_type=jnp.float32).reshape(degrees, channels, edge_count)
    weight = weight_mask.reshape(edge_count) * (1.0 / math.sqrt(slots))
    feat_float = features.astype(jnp.float32)
    messages = (radial * feat_float[None] * weight[None, None, :]).reshape(degrees, channels, slots, block_len)
    sphere_rows = sphere.reshape(degrees * degrees, slots, block_len)
    density = jnp.zeros((block_len,), jnp.float32)
    grad_msg = []
    grad_read = []
    for degree in range(degrees):
        part_y = sphere_rows[degree * degree:(degree + 1) * (degree + 1)]
        moment = jnp.einsum('kjp,cjp->kcp', part_y, messages[degree], precision=lax.Precision.HIGHEST)
        if degree == 0:
            density = density + lax.optimization_barrier(jnp.sum(readout[0][:, None] * moment[0], axis=0))
            grad_mom = jnp.broadcast_to(cot_block[None, None, :] * readout[0][None, :, None], moment.shape)
            grad_read.append(lax.optimization_barrier(jnp.sum(cot_block[None, :] * moment[0], axis=1)))
        else:
            squares = lax.optimization_barrier(jnp.sum(moment * moment, axis=0))
            density = density + lax.optimization_barrier(jnp.sum(readout[degree][:, None] * squares, axis=0))
            grad_mom = 2.0 * cot_block[None, None, :] * readout[degree][None, :, None] * moment
            grad_read.append(lax.optimization_barrier(jnp.sum(cot_block[None, :] * squares, axis=1)))
        grad_msg.append(jnp.einsum('kjp,kcp->cjp', part_y, grad_mom, precision=lax.Precision.HIGHEST))
    grad_messages = jnp.stack(grad_msg).reshape(degrees, channels, edge_count)
    grad_features = lax.optimization_barrier(jnp.sum(grad_messages * radial, axis=0)) * weight[None, :]
    grad_radial = (grad_messages * feat_float[None] * weight[None, None, :]).reshape(degrees * channels, edge_count).astype(jnp.bfloat16)
    grad_w2 = lax.dot_general(grad_radial, hidden, (((1,), (1,)), ((), ())), preferred_element_type=jnp.float32)
    grad_hidden = lax.dot_general(w_radial2, grad_radial, (((0,), (0,)), ((), ())), preferred_element_type=jnp.float32)
    logistic = jax.nn.sigmoid(preact)
    grad_pre = grad_hidden * logistic * (1.0 + preact * (1.0 - logistic))
    grad_w1 = lax.dot_general(grad_pre, radial_basis, (((1,), (1,)), ((), ())), precision=lax.Precision.HIGHEST)
    return (density, grad_features, grad_w1, grad_w2, jnp.stack(grad_read))

def reference(probe_pos, atom_pos, atom_feat, neighbours, valid, w_radial1, w_radial2, readout, cotangent):
    block_len = 128 if PROBE_DEV % 128 == 0 else PROBE_DEV
    count = PROBES // block_len
    probe_float = probe_pos.astype(jnp.float32)

    def advance(totals, number):
        grad_atoms, total_w1, total_w2, total_read = totals
        first_probe = number * block_len
        atom_rows = lax.dynamic_slice_in_dim(neighbours, first_probe, block_len, 1)
        mask_float = lax.dynamic_slice_in_dim(valid, first_probe, block_len, 1).astype(jnp.float32)
        probe_xyz = lax.dynamic_slice_in_dim(probe_float, first_probe, block_len, 1)
        cot_block = lax.dynamic_slice_in_dim(cotangent, first_probe, block_len, 0)
        flat_rows = atom_rows.reshape(-1)
        features = jnp.take(atom_feat, flat_rows, axis=1)
        atom_xyz = jnp.take(atom_pos, flat_rows, axis=1).astype(jnp.float32)
        probe_slab = (first_probe + jnp.arange(block_len, dtype=jnp.int32)) // PROBE_SLAB
        atom_slab = atom_rows // ATOM_SLAB
        offset = ((atom_slab - probe_slab[None, :] + 1) % N_SLAB - 1).astype(jnp.float32)
        density, grad_features, grad_w1, grad_w2, grad_read = probe_block(features, atom_xyz, probe_xyz, offset, mask_float, cot_block, w_radial1, w_radial2, readout)
        grad_atoms = grad_atoms.at[:, flat_rows].add(grad_features)
        return ((grad_atoms, total_w1 + grad_w1, total_w2 + grad_w2, total_read + grad_read), density)
    start_totals = (jnp.zeros((C, ATOMS), jnp.float32), jnp.zeros((RH, NB), jnp.float32), jnp.zeros((DEG * C, RH), jnp.float32), jnp.zeros((DEG, C), jnp.float32))
    totals, densities = lax.scan(advance, start_totals, jnp.arange(count, dtype=jnp.int32))
    scale = 1.0 / math.sqrt(PROBES)
    return (densities.reshape(-1), totals[0], totals[1] * scale, totals[2] * scale, totals[3] * scale)
```

```python
import functools
import math
import jax
import jax.numpy as jnp
import numpy as np
from jax import lax
from jax.experimental import pallas as pl
from jax.experimental.pallas import tpu as pltpu
from jax.sharding import Mesh
from jax.sharding import PartitionSpec as P

F32 = jnp.float32
BF16 = jnp.bfloat16
NT = (((1,), (1,)), ((), ()))
NN = (((1,), (0,)), ((), ()))
DEG_OF = [0] + [1] * 3 + [2] * 5 + [3] * 7 + [4] * 9
PACK_ROWS = 144
PAY_ROWS = 384


def dot(a, b, dims=NN):
    return lax.dot_general(a, b, dims, preferred_element_type=F32)


def harmonics(along_x, along_y, along_z):
    sq_x = along_x * along_x
    sq_y = along_y * along_y
    sq_z = along_z * along_z
    root3 = math.sqrt(3.0)
    root15 = math.sqrt(15.0)
    root5 = math.sqrt(5.0)
    coef_a1 = math.sqrt(35.0 / 8.0)
    coef_a2 = math.sqrt(105.0)
    coef_a3 = math.sqrt(21.0 / 8.0)
    coef_a4 = math.sqrt(7.0) / 2.0
    coef_b1 = 3.0 * math.sqrt(35.0) / 2.0
    coef_b2 = 3.0 * math.sqrt(70.0) / 4.0
    coef_b3 = 3.0 * math.sqrt(5.0) / 2.0
    coef_b4 = 3.0 * math.sqrt(10.0) / 4.0
    return [
        jnp.ones_like(along_x),
        root3 * along_y,
        root3 * along_z,
        root3 * along_x,
        root15 * along_x * along_y,
        root15 * along_y * along_z,
        root5 / 2.0 * (3.0 * sq_z - 1.0),
        root15 * along_x * along_z,
        root15 / 2.0 * (sq_x - sq_y),
        coef_a1 * along_y * (3.0 * sq_x - sq_y),
        coef_a2 * along_x * along_y * along_z,
        coef_a3 * along_y * (5.0 * sq_z - 1.0),
        coef_a4 * along_z * (5.0 * sq_z - 3.0),
        coef_a3 * along_x * (5.0 * sq_z - 1.0),
        coef_a2 / 2.0 * along_z * (sq_x - sq_y),
        coef_a1 * along_x * (sq_x - 3.0 * sq_y),
        coef_b1 * along_x * along_y * (sq_x - sq_y),
        coef_b2 * along_y * along_z * (3.0 * sq_x - sq_y),
        coef_b3 * along_x * along_y * (7.0 * sq_z - 1.0),
        coef_b4 * along_y * along_z * (7.0 * sq_z - 3.0),
        0.375 * (35.0 * sq_z * sq_z - 30.0 * sq_z + 3.0),
        coef_b4 * along_x * along_z * (7.0 * sq_z - 3.0),
        coef_b3 / 2.0 * (sq_x - sq_y) * (7.0 * sq_z - 1.0),
        coef_b2 * along_x * along_z * (sq_x - 3.0 * sq_y),
        coef_b1 / 4.0 * (sq_x * (sq_x - 3.0 * sq_y) - sq_y * (3.0 * sq_x - sq_y)),
    ]


def iota(shape, dim):
    return lax.broadcasted_iota(jnp.int32, shape, dim)


def kernel(
    low_ref, own_ref, high_ref, idx_ref, wgt_ref, probe_ref, cot_ref, w1_ref, w2_ref, w2t_ref, ro_ref,
    dens_ref, gwin_ref, pay_ref,
    oh_ref, feat_ref, pos_ref, sph_ref, rad_ref, sb_ref, dens_s, gro_s, gwin_s, gw2_s, gw1_s, radial_s, gr_s,
    *, unroll_a, unroll_c,
):
    groups = idx_ref.shape[0]

    def gather(g, carry):
        row = idx_ref[pl.ds(g, 1), :]
        total = None
        for part, src in enumerate((low_ref, own_ref, high_ref)):
            hot = jnp.where(iota((256, 256), 0) + 256 * part == row, 1.0, 0.0).astype(BF16)
            oh_ref[g, pl.ds(256 * part, 256), :] = hot
            piece = dot(src[...], hot)
            total = piece if total is None else total + piece
        feat_ref[g] = total[:128].astype(BF16)
        for i in range(3):
            pos_ref[i, pl.ds(g, 1), :] = total[128 + i : 129 + i]
        return carry

    lax.fori_loop(0, groups, gather, 0, unroll=unroll_a)

    dx = pos_ref[0] - probe_ref[0]
    dy = pos_ref[1] - probe_ref[1]
    idx = idx_ref[...]
    offset = (idx >= 256).astype(F32) + (idx >= 512).astype(F32) - 1.0
    dz = pos_ref[2] + 2.0 * offset - probe_ref[2]
    radius = jnp.sqrt(dx * dx + dy * dy + dz * dz + 0.25)
    rad_ref[...] = radius
    inv = 1.0 / radius
    for k, val in enumerate(harmonics(dx * inv, dy * inv, dz * inv)):
        top = val.astype(BF16).astype(F32)
        sph_ref[0, k] = top
        sph_ref[1, k] = val - top

    sb_ref[...] = jnp.zeros_like(sb_ref)
    gro_s[...] = jnp.zeros_like(gro_s)
    gwin_s[...] = jnp.zeros_like(gwin_s)
    gw2_s[...] = jnp.zeros_like(gw2_s)
    gw1_s[...] = jnp.zeros_like(gw1_s)

    w1 = w1_ref[...]
    w1_top = w1.astype(BF16).astype(F32)
    w1_cat = jnp.concatenate([w1_top, w1_top, w1 - w1_top, jnp.zeros_like(w1)], axis=1).astype(BF16)

    def block(g, carry):
        wgt = wgt_ref[pl.ds(g, 1), :]
        offs = rad_ref[pl.ds(g, 1), :] - 0.75 * iota((8, 256), 0).astype(F32)
        basis = jnp.exp(-2.0 * offs * offs)
        basis_top = basis.astype(BF16).astype(F32)
        basis_cat = jnp.concatenate(
            [basis_top, basis - basis_top, basis_top, jnp.zeros_like(basis)], axis=0
        ).astype(BF16)
        preact = dot(w1_cat, basis_cat)
        sig = 1.0 / (1.0 + jnp.exp(-preact))
        hidden = (preact * sig).astype(BF16)
        slope = sig * (1.0 + preact * (1.0 - sig))
        mask = iota((8, 256), 0) == iota((8, 256), 1) // 32
        zero8 = jnp.zeros((8, 256), F32)
        for half in range(2):
            def rows_of(k):
                return jnp.where(mask, sph_ref[half, k, pl.ds(g, 1), :], 0.0)

            for k in range(0, 24, 2):
                base = 128 * half + (8 * k if k < 16 else 8 * (k - 16))
                la, lb = DEG_OF[k], DEG_OF[k + 1]
                a, b = rows_of(k), rows_of(k + 1)
                if la == lb:
                    sb_ref[la, pl.ds(base, 16), :] = jnp.concatenate([a, b], axis=0).astype(BF16)
                else:
                    sb_ref[la, pl.ds(base, 16), :] = jnp.concatenate([a, zero8], axis=0).astype(BF16)
                    sb_ref[lb, pl.ds(base, 16), :] = jnp.concatenate([zero8, b], axis=0).astype(BF16)
            sb_ref[4, pl.ds(128 * half + 64, 16), :] = jnp.concatenate([rows_of(24), zero8], axis=0).astype(BF16)
        fw = feat_ref[g].astype(F32) * wgt
        mom_a = None
        for l in range(5):
            radial = dot(w2_ref[pl.ds(128 * l, 128), :], hidden)
            radial_s[l] = radial
            piece = dot((radial * fw).astype(BF16), sb_ref[l], NT)
            if l == 4:
                mom_b = piece
            else:
                mom_a = piece if mom_a is None else mom_a + piece
        mom_a = mom_a[:, :128] + mom_a[:, 128:]
        mom_b = mom_b[:, :128] + mom_b[:, 128:]
        cot = cot_ref[pl.ds(g, 1), :][:, :128]
        first = iota((128, 128), 1) < 8
        ro_a, ro_b = ro_ref[:, :128], ro_ref[:, 128:]
        sq_a = jnp.where(first, mom_a, mom_a * mom_a)
        sq_b = mom_b * mom_b
        dens_s[pl.ds(g, 1), :] = jnp.concatenate(
            [jnp.sum(sq_a * ro_a, axis=0, keepdims=True), jnp.sum(sq_b * ro_b, axis=0, keepdims=True)], axis=1
        )
        gro_s[:, :128] += sq_a * cot
        gro_s[:, 128:] += sq_b * cot
        gm_a = (jnp.where(first, 1.0, 2.0 * mom_a) * (ro_a * cot)).astype(BF16)
        gm_b = (2.0 * mom_b * (ro_b * cot)).astype(BF16)
        gm_a = jnp.concatenate([gm_a, gm_a], axis=1)
        gm_b = jnp.concatenate([gm_b, gm_b], axis=1)
        gf = None
        for l in range(5):
            gmsg = dot(gm_b if l == 4 else gm_a, sb_ref[l])
            piece = gmsg * radial_s[l]
            gf = piece if gf is None else gf + piece
            gr_s[pl.ds(128 * l, 128), :] = (gmsg * fw).astype(BF16)
        gf = (gf * wgt).astype(BF16)
        gwin_s[...] += dot(gf, oh_ref[g], NT)
        gr = gr_s[...]
        gw2_s[...] += dot(hidden, gr, NT)
        gpre = dot(w2t_ref[...], gr) * slope
        gw1_s[...] += dot(basis_cat, gpre.astype(BF16), NT)
        return carry

    lax.fori_loop(0, groups, block, 0, unroll=unroll_c)

    hi = lax.Precision.HIGHEST
    fold = jnp.where(iota((256, 128), 0) % 8 == iota((256, 128), 1), 1.0, 0.0)
    dens_ref[...] = lax.dot_general(dens_s[...], fold, NN, precision=hi, preferred_element_type=F32)
    for part in range(3):
        gwin_ref[part] = gwin_s[:, pl.ds(256 * part, 256)].astype(BF16)
    for l in range(5):
        pay_ref[pl.ds(64 * l, 64), :] = gw2_s[:, pl.ds(128 * l, 128)].astype(pay_ref.dtype)
    k_of = iota((8, 256), 1) // 8
    deg = (k_of >= 1).astype(jnp.int32) + (k_of >= 4) + (k_of >= 9) + (k_of >= 16)
    pick = jnp.where((iota((8, 256), 0) == deg) & (k_of < 25), 1.0, 0.0)
    gro = lax.dot_general(pick, gro_s[...], NT, precision=hi, preferred_element_type=F32)
    gw1 = gw1_s[:8, :] + gw1_s[8:16, :]
    gw1 = jnp.concatenate([gw1, jnp.zeros((8, 64), F32)], axis=1)
    pay_ref[pl.ds(320, 16), :] = jnp.concatenate([gro, gw1], axis=0).astype(pay_ref.dtype)
    pay_ref[pl.ds(336, 48), :] = jnp.zeros((48, 128), pay_ref.dtype)


def layer(low, own, high, idx, wgt, probe, cot, w1, w2, w2t, ro, unroll_a=2, unroll_c=1, pay_dtype=BF16):
    groups = idx.shape[0]
    return pl.pallas_call(
        functools.partial(kernel, unroll_a=unroll_a, unroll_c=unroll_c),
        out_shape=(
            jax.ShapeDtypeStruct((groups, 128), F32),
            jax.ShapeDtypeStruct((3, 128, 256), BF16),
            jax.ShapeDtypeStruct((PAY_ROWS, 128), pay_dtype),
        ),
        in_specs=[pl.BlockSpec(memory_space=pltpu.VMEM)] * 11,
        out_specs=[pl.BlockSpec(memory_space=pltpu.VMEM)] * 3,
        scratch_shapes=[
            pltpu.VMEM((groups, 768, 256), BF16),
            pltpu.VMEM((groups, 128, 256), BF16),
            pltpu.VMEM((3, groups, 256), F32),
            pltpu.VMEM((2, 25, groups, 256), F32),
            pltpu.VMEM((groups, 256), F32),
            pltpu.VMEM((5, 256, 256), BF16),
            pltpu.VMEM((groups, 256), F32),
            pltpu.VMEM((128, 256), F32),
            pltpu.VMEM((128, 768), F32),
            pltpu.VMEM((64, 640), F32),
            pltpu.VMEM((32, 64), F32),
            pltpu.VMEM((5, 128, 256), F32),
            pltpu.VMEM((640, 256), BF16),
        ],
        compiler_params=pltpu.CompilerParams(vmem_limit_bytes=40 << 20),
        name="probe_layer",
    )(low, own, high, idx, wgt, probe, cot, w1, w2, w2t, ro)


def prep(neighbours, valid, probe_pos, cotangent, readout, slab_index, slab_count, atom_slab):
    slots, probes = neighbours.shape
    groups = probes // 8
    idx = (neighbours - (slab_index - 1) * atom_slab) % (slab_count * atom_slab)
    idx = idx.T.reshape(groups, 8 * slots)
    wgt = (valid.astype(F32) * (1.0 / math.sqrt(slots))).T.reshape(groups, 8 * slots)
    probe = jnp.repeat(probe_pos.astype(F32).reshape(3, groups, 8), slots, axis=2)
    cot = jnp.tile(cotangent.reshape(groups, 1, 8), (1, 32, 1)).reshape(groups, 256)
    deg = jnp.array(DEG_OF + [5] * 7)
    pick = (deg[None, :] == jnp.arange(5)[:, None]).astype(F32)
    pick = jnp.repeat(pick, 8, axis=1)
    ro = jnp.einsum("lc,lk->ck", readout, pick, precision=lax.Precision.HIGHEST)
    return idx, wgt, probe, cot, ro


AXES = ("z", "ylo", "x", "core", "yhi")
SLAB = ("z", "ylo", "x", "core")
NEAR = ("ylo", "x", "core")
FAR = ("z", "yhi")


def spread_kernel(x_ref, o_ref):
    total = jnp.sum(x_ref[...].astype(F32), axis=0)
    o_ref[...] = jnp.broadcast_to(total[None], o_ref.shape).astype(o_ref.dtype)


def spread(x, copies):
    return pl.pallas_call(
        spread_kernel,
        out_shape=jax.ShapeDtypeStruct((copies,) + x.shape[1:], x.dtype),
        in_specs=[pl.BlockSpec(memory_space=pltpu.VMEM)],
        out_specs=pl.BlockSpec(memory_space=pltpu.VMEM),
        name="spread",
    )(x)


def finish_kernel(scale, x_ref, w1_ref, w2_ref, ro_ref):
    def part(start, rows):
        return x_ref[pl.ds(start, rows), :].astype(F32) * scale

    for l in range(5):
        w2_ref[pl.ds(128 * l, 128), :] = part(64 * l, 64).T
    ro_ref[...] = part(320, 8)[:5]
    w1_ref[...] = part(328, 8).T[:64]


def finish(x, scale):
    return pl.pallas_call(
        functools.partial(finish_kernel, scale),
        out_shape=(
            jax.ShapeDtypeStruct((64, 8), F32),
            jax.ShapeDtypeStruct((640, 64), F32),
            jax.ShapeDtypeStruct((5, 128), F32),
        ),
        in_specs=[pl.BlockSpec(memory_space=pltpu.VMEM)],
        out_specs=[pl.BlockSpec(memory_space=pltpu.VMEM)] * 3,
        name="finish",
    )(x)


def exchange(x, axes):
    return lax.all_to_all(x, axes, 0, 0, tiled=True)


def passed_along(block, distance):
    count = lax.axis_size(SLAB)
    return lax.ppermute(block, SLAB, [(i, (i + distance) % count) for i in range(count)])


def shards(probe_pos, atom_pos, atom_feat, neighbours, valid, w_radial1, w_radial2, readout, cotangent):
    slab_count = lax.axis_size(SLAB)
    slab_index = lax.axis_index(SLAB)
    planes = lax.axis_size("yhi")
    atom_dev = atom_feat.shape[1]
    atom_slab = atom_dev * planes
    pack = jnp.concatenate(
        [atom_feat, atom_pos, jnp.zeros((PACK_ROWS - 131, atom_dev), BF16)], axis=0
    )
    own = lax.all_gather(pack, "yhi", axis=1, tiled=True)
    low = passed_along(own, 1)
    high = passed_along(own, -1)
    idx, wgt, probe, cot, ro = prep(
        neighbours, valid, probe_pos, cotangent, readout, slab_index, slab_count, atom_slab
    )
    dens, gwin, pay = layer(
        low, own, high, idx, wgt, probe, cot, w_radial1, w_radial2, w_radial2.T, ro
    )
    density = dens[:, :8].reshape(-1)
    from_high = passed_along(gwin[0], -1)
    from_low = passed_along(gwin[2], 1)
    near, far = lax.axis_size(NEAR), lax.axis_size(FAR)
    part = exchange(pay.reshape(near, PAY_ROWS // near, 128), NEAR)
    part = exchange(spread(part, far), FAR)
    slab_sum = gwin[1].astype(F32) + from_high.astype(F32) + from_low.astype(F32)
    plane = lax.axis_index("yhi")
    mine = lax.dynamic_slice_in_dim(slab_sum, plane * atom_dev, atom_dev, 1)
    other = lax.dynamic_slice_in_dim(slab_sum, (1 - plane) * atom_dev, atom_dev, 1)
    got = lax.ppermute(other.astype(BF16), "yhi", [(0, 1), (1, 0)])
    grad_feat = mine + got.astype(F32)
    part = exchange(spread(part, near), NEAR)
    scale = 1.0 / math.sqrt(neighbours.shape[1] * slab_count * planes)
    grad_w1, grad_w2, grad_ro = finish(part.reshape(PAY_ROWS, 128), scale)
    return density, grad_feat, grad_w1, grad_w2, grad_ro


def solution(mesh):
    fine = Mesh(np.asarray(mesh.devices).reshape(8, 2, 4, 2, 2), AXES)
    flat = P(None, AXES)
    in_specs = (flat, flat, flat, flat, flat, P(), P(), P(), P(AXES))
    out_specs = (P(AXES), flat, P(), P(), P())
    return jax.shard_map(shards, mesh=fine, in_specs=in_specs, out_specs=out_specs, check_vma=False)
```

```python
import functools
import math
import jax
import jax.numpy as jnp
import numpy as np
from jax import lax
from jax.experimental import pallas as pl
from jax.experimental.pallas import tpu as pltpu
from jax.sharding import Mesh
from jax.sharding import PartitionSpec as P

F32 = jnp.float32
BF16 = jnp.bfloat16
WIRES = (F32, F32, F32)
PINNED = 0
NT = (((1,), (1,)), ((), ()))
NN = (((1,), (0,)), ((), ()))
DEG_OF = [0] + [1] * 3 + [2] * 5 + [3] * 7 + [4] * 9
PACK_ROWS = 144
PAY_ROWS = 384


def dot(a, b, dims=NN):
    return lax.dot_general(a, b, dims, preferred_element_type=F32)


def harmonics(along_x, along_y, along_z):
    sq_x = along_x * along_x
    sq_y = along_y * along_y
    sq_z = along_z * along_z
    root3 = math.sqrt(3.0)
    root15 = math.sqrt(15.0)
    root5 = math.sqrt(5.0)
    coef_a1 = math.sqrt(35.0 / 8.0)
    coef_a2 = math.sqrt(105.0)
    coef_a3 = math.sqrt(21.0 / 8.0)
    coef_a4 = math.sqrt(7.0) / 2.0
    coef_b1 = 3.0 * math.sqrt(35.0) / 2.0
    coef_b2 = 3.0 * math.sqrt(70.0) / 4.0
    coef_b3 = 3.0 * math.sqrt(5.0) / 2.0
    coef_b4 = 3.0 * math.sqrt(10.0) / 4.0
    return [
        jnp.ones_like(along_x),
        root3 * along_y,
        root3 * along_z,
        root3 * along_x,
        root15 * along_x * along_y,
        root15 * along_y * along_z,
        root5 / 2.0 * (3.0 * sq_z - 1.0),
        root15 * along_x * along_z,
        root15 / 2.0 * (sq_x - sq_y),
        coef_a1 * along_y * (3.0 * sq_x - sq_y),
        coef_a2 * along_x * along_y * along_z,
        coef_a3 * along_y * (5.0 * sq_z - 1.0),
        coef_a4 * along_z * (5.0 * sq_z - 3.0),
        coef_a3 * along_x * (5.0 * sq_z - 1.0),
        coef_a2 / 2.0 * along_z * (sq_x - sq_y),
        coef_a1 * along_x * (sq_x - 3.0 * sq_y),
        coef_b1 * along_x * along_y * (sq_x - sq_y),
        coef_b2 * along_y * along_z * (3.0 * sq_x - sq_y),
        coef_b3 * along_x * along_y * (7.0 * sq_z - 1.0),
        coef_b4 * along_y * along_z * (7.0 * sq_z - 3.0),
        0.375 * (35.0 * sq_z * sq_z - 30.0 * sq_z + 3.0),
        coef_b4 * along_x * along_z * (7.0 * sq_z - 3.0),
        coef_b3 / 2.0 * (sq_x - sq_y) * (7.0 * sq_z - 1.0),
        coef_b2 * along_x * along_z * (sq_x - 3.0 * sq_y),
        coef_b1 / 4.0 * (sq_x * (sq_x - 3.0 * sq_y) - sq_y * (3.0 * sq_x - sq_y)),
    ]


def iota(shape, dim):
    return lax.broadcasted_iota(jnp.int32, shape, dim)


VMEM_SPEC = pl.BlockSpec(memory_space=pltpu.VMEM)


def tables_kernel(place_ref, nb_ref, valid_ref, probe_ref, tab_ref):
    slots, probes = nb_ref.shape
    groups = probes // 8
    atoms = place_ref[2]
    idx = nb_ref[...] - place_ref[0]
    idx = jnp.where(idx < 0, idx + atoms, jnp.where(idx >= atoms, idx - atoms, idx))
    idx = idx ^ place_ref[1]
    spot = (iota((probes, 256), 1) // 32) == (iota((probes, 256), 0) & 7)

    def grouped(wide):
        return jnp.sum(jnp.where(spot, wide, 0.0).reshape(groups, 8, 256), axis=1)

    tile = jnp.where((iota((slots, 256), 1) & 31) == iota((slots, 256), 0), 1.0, 0.0).astype(BF16)

    def spread_slots(x):
        return grouped(dot(x.astype(F32).T.astype(BF16), tile))

    tab_ref[0] = 256.0 * spread_slots(idx >> 8) + spread_slots(idx & 255)
    tab_ref[1] = spread_slots(valid_ref[...]) * (1.0 / math.sqrt(slots))
    pos = jnp.concatenate([probe_ref[...].astype(F32), jnp.zeros((5, probes), F32)], axis=0).T
    for i in range(3):
        tab_ref[2 + i] = grouped(jnp.broadcast_to(pos[:, i : i + 1], (probes, 256)))


def tables(place, neighbours, valid, probe_pos):
    groups = neighbours.shape[1] // 8
    return pl.pallas_call(
        tables_kernel,
        out_shape=jax.ShapeDtypeStruct((5, groups, 256), F32),
        in_specs=[pl.BlockSpec(memory_space=pltpu.SMEM)] + [VMEM_SPEC] * 3,
        out_specs=VMEM_SPEC,
        compiler_params=pltpu.CompilerParams(vmem_limit_bytes=8 << 20),
        name="tables",
    )(place, neighbours, valid, probe_pos)


def hot_rows(row, part):
    return jnp.where((iota((256, 256), 0) + 256 * part).astype(F32) == row, 1.0, 0.0).astype(BF16)


def kernel(
    b0, b1, b2, b3, b4, b5, tab_ref, w1t_ref, w2t_ref, ro_ref, cot_ref,
    dens_ref, gf_ref, pay_ref,
    win_ref, feat_ref, pos_ref, sph_ref, rad_ref, w2_ref, cotb_ref, dens_s, gro_s, radial_s,
    hid_ref, slope_ref, bas_ref, gr_ref,
    *, ua, ub, uc, lock,
):
    groups = tab_ref.shape[1]

    def lanes(g):
        return pl.ds(pl.multiple_of(g * 256, 256), 256)

    for i, src in enumerate((b0, b1, b2, b3, b4, b5)):
        win_ref[:, pl.ds(128 * i, 128)] = src[...]
    for l in range(5):
        w2_ref[l] = w2t_ref[:, pl.ds(128 * l, 128)].astype(F32).T.astype(BF16)
    cotb_ref[...] = jnp.broadcast_to(cot_ref[...], (128, 128)).T

    def gather(g, carry):
        row = tab_ref[0, pl.ds(g, 1), :]
        total = None
        for part in range(3):
            piece = dot(win_ref[:, pl.ds(256 * part, 256)], hot_rows(row, part))
            total = piece if total is None else total + piece
        feat_ref[:, lanes(g)] = total[:128].astype(BF16)
        for i in range(3):
            pos_ref[i, pl.ds(g, 1), :] = total[128 + i : 129 + i]
        return carry

    lax.fori_loop(0, groups, gather, 0, unroll=ua)

    idx = tab_ref[0]
    offset = (idx >= 256.0).astype(F32) + (idx >= 512.0).astype(F32) - 1.0
    dx = pos_ref[0] - tab_ref[2]
    dy = pos_ref[1] - tab_ref[3]
    dz = pos_ref[2] + 2.0 * offset - tab_ref[4]
    radius = jnp.sqrt(dx * dx + dy * dy + dz * dz + 0.25)
    rad_ref[...] = radius
    inv = 1.0 / radius
    for k, val in enumerate(harmonics(dx * inv, dy * inv, dz * inv)):
        top = val.astype(BF16).astype(F32)
        sph_ref[0, k] = top
        sph_ref[1, k] = val - top

    gro_s[...] = jnp.zeros_like(gro_s)

    w1 = w1t_ref[...].T
    w1_top = w1.astype(BF16).astype(F32)
    w1_cat = jnp.concatenate([w1_top, w1_top, w1 - w1_top, jnp.zeros_like(w1)], axis=1).astype(BF16)

    def network(g, carry):
        offs = rad_ref[pl.ds(g, 1), :] - 0.75 * iota((8, 256), 0).astype(F32)
        basis = jnp.exp(-2.0 * offs * offs)
        basis_top = basis.astype(BF16).astype(F32)
        basis_cat = jnp.concatenate(
            [basis_top, basis - basis_top, basis_top, jnp.zeros_like(basis)], axis=0
        ).astype(BF16)
        bas_ref[:, lanes(g)] = basis_cat
        preact = dot(w1_cat, basis_cat)
        sig = 1.0 / (1.0 + jnp.exp(-preact))
        hid_ref[:, lanes(g)] = (preact * sig).astype(BF16)
        slope_ref[:, lanes(g)] = sig * (1.0 + preact * (1.0 - sig))
        return carry

    lax.fori_loop(0, groups, network, 0, unroll=ub)

    mask = iota((8, 256), 0) == iota((8, 256), 1) // 32

    def spheres(g):
        tops, lows = [], []
        for l in range(5):
            for half, out in ((0, tops), (1, lows)):
                rows = [
                    jnp.where(mask, sph_ref[half, k, pl.ds(g, 1), :], 0.0)
                    for k in range(l * l, (l + 1) * (l + 1))
                ]
                out.append(jnp.concatenate(rows, axis=0) if len(rows) > 1 else rows[0])
        return tops, lows

    def forward(g, u, sph):
        tops, lows = sph
        fw = feat_ref[:, lanes(g)].astype(F32) * tab_ref[1, pl.ds(g, 1), :]
        hidden = hid_ref[:, lanes(g)]
        msgs = []
        for l in range(5):
            radial = dot(w2_ref[l], hidden)
            radial_s[u, l] = radial
            msgs.append((radial * fw).astype(BF16))
        moms = []
        for degs in ((0, 1), (2, 3), (4,)):
            rows = jnp.concatenate([x for l in degs for x in (tops[l], lows[l])], axis=0).astype(BF16)
            right = jnp.concatenate([msgs[l] for l in degs], axis=0) if len(degs) > 1 else msgs[degs[0]]
            out = dot(rows, right, NT)
            at = 0
            for i, l in enumerate(degs):
                size = 8 * (2 * l + 1)
                cols = slice(128 * i, 128 * i + 128)
                moms.append(out[at : at + size, cols] + out[at + size : at + 2 * size, cols])
                at += 2 * size
        return moms

    def middle(g, moms):
        cot = cotb_ref[pl.ds(pl.multiple_of(g * 8, 8), 8), :]
        dens = None
        grads = []
        for l, mom in enumerate(moms):
            ro = ro_ref[pl.ds(l, 1), :]
            parts = [mom[8 * i : 8 * i + 8] for i in range(2 * l + 1)]
            if l == 0:
                squares = parts[0]
                grads.append(cot * ro)
            else:
                squares = None
                for x in parts:
                    squares = x * x if squares is None else squares + x * x
                fac = 2.0 * cot * ro
                grads.append(jnp.concatenate([x * fac for x in parts], axis=0))
            dens = squares * ro if dens is None else dens + squares * ro
            gro_s[l] += squares * cot
        dens_s[pl.ds(pl.multiple_of(g * 8, 8), 8), :] = dens
        return grads

    def backward(g, u, sph, grads):
        tops, lows = sph
        wgt = tab_ref[1, pl.ds(g, 1), :]
        fw = feat_ref[:, lanes(g)].astype(F32) * wgt
        gf = None
        for l in range(5):
            top = grads[l].astype(BF16).astype(F32)
            left = jnp.concatenate([top, top, grads[l] - top], axis=0).T.astype(BF16)
            right = jnp.concatenate([tops[l], lows[l], tops[l]], axis=0).astype(BF16)
            gmsg = dot(left, right)
            piece = gmsg * radial_s[u, l]
            gf = piece if gf is None else gf + piece
            gr_ref[pl.ds(128 * l, 128), lanes(g)] = (gmsg * fw).astype(BF16)
        gf_ref[:, lanes(g)] = (gf * wgt).astype(BF16)

    def block(i, carry):
        gs = [i * lock + u for u in range(lock)]
        sphs = [spheres(g) for g in gs]
        moms = [forward(g, u, sphs[u]) for u, g in enumerate(gs)]
        grads = [middle(g, moms[u]) for u, g in enumerate(gs)]
        for u, g in enumerate(gs):
            backward(g, u, sphs[u], grads[u])
        return carry

    lax.fori_loop(0, groups // lock, block, 0, unroll=uc)

    hid = hid_ref[...]
    gr = gr_ref[...]
    for l in range(5):
        pay_ref[pl.ds(64 * l, 64), :] = dot(hid, gr_ref[pl.ds(128 * l, 128), :], NT).astype(pay_ref.dtype)
    gpre = (dot(w2t_ref[...], gr) * slope_ref[...]).astype(BF16)
    gw1 = dot(bas_ref[...], gpre, NT)
    gw1 = gw1[:8, :] + gw1[8:16, :]
    gw1 = jnp.concatenate([gw1, jnp.zeros((8, 64), F32)], axis=1)
    gro = jnp.concatenate(
        [jnp.sum(gro_s[l], axis=0, keepdims=True) for l in range(5)] + [jnp.zeros((3, 128), F32)], axis=0
    )
    pay_ref[pl.ds(320, 16), :] = jnp.concatenate([gro, gw1], axis=0).astype(pay_ref.dtype)
    pay_ref[pl.ds(336, 48), :] = jnp.zeros((48, 128), pay_ref.dtype)
    dens_ref[...] = lax.dot_general(
        jnp.ones((8, 128), F32), dens_s[...], NT, precision=lax.Precision.HIGHEST, preferred_element_type=F32
    )


def scatter_kernel(gf_ref, tab_ref, *outs):
    groups = tab_ref.shape[1]
    for part in range(3):
        total = None
        for g in range(groups):
            row = tab_ref[0, pl.ds(g, 1), :]
            piece = dot(gf_ref[:, pl.ds(256 * g, 256)], hot_rows(row, part), NT)
            total = piece if total is None else total + piece
        total = total.astype(BF16)
        outs[part][:128] = total[:, :128]
        outs[part][128:] = total[:, 128:]


def scatter(gf, tab):
    return pl.pallas_call(
        scatter_kernel,
        out_shape=(jax.ShapeDtypeStruct((256, 128), BF16),) * 3,
        in_specs=[VMEM_SPEC] * 2,
        out_specs=[VMEM_SPEC] * 3,
        compiler_params=pltpu.CompilerParams(vmem_limit_bytes=16 << 20),
        name="scatter_feat",
    )(gf, tab)


def layer(blocks, tab, w1t, w2t, ro, cot, ua=8, ub=8, uc=1, lock=4):
    groups = tab.shape[1]
    edges = groups * 256
    return pl.pallas_call(
        functools.partial(kernel, ua=ua, ub=ub, uc=uc, lock=lock),
        out_shape=(
            jax.ShapeDtypeStruct((8, 128), F32),
            jax.ShapeDtypeStruct((128, edges), BF16),
            jax.ShapeDtypeStruct((PAY_ROWS, 128), WIRES[0]),
        ),
        in_specs=[VMEM_SPEC] * 11,
        out_specs=[VMEM_SPEC] * 3,
        scratch_shapes=[
            pltpu.VMEM((PACK_ROWS, 768), BF16),
            pltpu.VMEM((128, edges), BF16),
            pltpu.VMEM((3, groups, 256), F32),
            pltpu.VMEM((2, 25, groups, 256), F32),
            pltpu.VMEM((groups, 256), F32),
            pltpu.VMEM((5, 128, 64), BF16),
            pltpu.VMEM((128, 128), F32),
            pltpu.VMEM((128, 128), F32),
            pltpu.VMEM((5, 8, 128), F32),
            pltpu.VMEM((lock, 5, 128, 256), F32),
            pltpu.VMEM((64, edges), BF16),
            pltpu.VMEM((64, edges), F32),
            pltpu.VMEM((32, edges), BF16),
            pltpu.VMEM((640, edges), BF16),
        ],
        compiler_params=pltpu.CompilerParams(vmem_limit_bytes=32 << 20),
        name="probe_layer",
    )(*blocks, tab, w1t, w2t, ro, cot)


def finish_kernel(scale, x_ref, w1_ref, w2_ref, ro_ref):
    for l in range(5):
        w2_ref[:, pl.ds(128 * l, 128)] = x_ref[pl.ds(64 * l, 64), :] * scale
    ro_ref[...] = x_ref[pl.ds(320, 8), :][:5] * scale
    w1_ref[...] = x_ref[pl.ds(328, 8), :][:, :64] * scale


def finish(x, scale):
    return pl.pallas_call(
        functools.partial(finish_kernel, scale),
        out_shape=(
            jax.ShapeDtypeStruct((8, 64), F32),
            jax.ShapeDtypeStruct((64, 640), F32),
            jax.ShapeDtypeStruct((5, 128), F32),
        ),
        in_specs=[VMEM_SPEC],
        out_specs=[VMEM_SPEC] * 3,
        compiler_params=pltpu.CompilerParams(vmem_limit_bytes=8 << 20),
        name="finish",
    )(x)


AXES = ("z", "ylo", "x", "core", "yhi")
SLAB = ("z", "ylo", "x", "core")
NEAR = ("ylo", "x", "core")
FAR = ("z", "yhi")


def exchange(x, axes):
    return lax.all_to_all(x, axes, 0, 0, tiled=True)


def passed_along(block, distance):
    count = lax.axis_size(SLAB)
    return lax.ppermute(block, SLAB, [(i, (i + distance) % count) for i in range(count)])


def sent(block, slab_step, plane_step):
    slabs, planes = lax.axis_size(SLAB), lax.axis_size("yhi")
    route = [
        (s * planes + p, (s + slab_step) % slabs * planes + (p + plane_step) % planes)
        for s in range(slabs)
        for p in range(planes)
    ]
    return lax.ppermute(block, AXES, route)


def joined(mine, other):
    even = lax.axis_index("yhi") == 0
    return jnp.concatenate([jnp.where(even, mine, other), jnp.where(even, other, mine)], axis=1)


def totals(x, copies, wire):
    total = jnp.sum(x.astype(F32), axis=0).astype(wire)
    return jnp.broadcast_to(total[None], (copies,) + total.shape)


def shards(probe_pos, atom_pos, atom_feat, neighbours, valid, w_radial1, w_radial2, readout, cotangent):
    slab_count = lax.axis_size(SLAB)
    slab_index = lax.axis_index(SLAB)
    planes = lax.axis_size("yhi")
    plane = lax.axis_index("yhi")
    atom_dev = atom_feat.shape[1]
    atom_slab = atom_dev * planes
    pack = jnp.concatenate(
        [atom_feat, atom_pos, jnp.zeros((PACK_ROWS - 131, atom_dev), BF16)], axis=0
    )
    steps = ((-1, 0), (-1, 1), (0, 0), (0, 1), (1, 0), (1, 1))
    blocks = [pack if step == (0, 0) else sent(pack, -step[0], step[1]) for step in steps]
    place = jnp.stack(
        [(slab_index - 1) * atom_slab, plane * atom_dev, jnp.full((), slab_count * atom_slab, jnp.int32)]
    )
    tab = tables(place, neighbours, valid, probe_pos)
    dens, edge_grad, pay = layer(
        blocks, tab, w_radial1.T, w_radial2.T, readout, cotangent.reshape(1, -1)
    )
    density = dens[0]
    near, far = lax.axis_size(NEAR), lax.axis_size(FAR)
    part = exchange(pay.reshape(near, PAY_ROWS // near, 128).astype(WIRES[0]), NEAR)
    to_low, own_grad, to_high = scatter(edge_grad, tab)
    wide = totals(part, far, WIRES[1])
    if PINNED:
        wide, to_low, to_high = lax.optimization_barrier((wide, to_low, to_high))
    part = exchange(wide, FAR)
    from_high = passed_along(to_low, -1)
    from_low = passed_along(to_high, 1)
    slab_sum = own_grad.astype(F32) + from_high.astype(F32) + from_low.astype(F32)
    wide = totals(part, near, WIRES[2])
    other = slab_sum[atom_dev:].astype(BF16)
    if PINNED > 1:
        wide, other = lax.optimization_barrier((wide, other))
    part = exchange(wide, NEAR)
    grad_feat = slab_sum[:atom_dev] + sent(other, 0, 1).astype(F32)
    scale = 1.0 / math.sqrt(neighbours.shape[1] * slab_count * planes)
    w1t, w2t, grad_ro = finish(part.reshape(PAY_ROWS, 128), scale)
    grad_w1, grad_w2 = w1t.T, w2t.T
    return density, grad_feat, grad_w1, grad_w2, grad_ro


def solution(mesh):
    fine = Mesh(np.asarray(mesh.devices).reshape(8, 2, 4, 2, 2), AXES)
    flat = P(None, AXES)
    in_specs = (flat, flat, flat, flat, flat, P(), P(), P(), P(AXES))
    out_specs = (P(AXES), flat, P(), P(), P())
    return jax.shard_map(shards, mesh=fine, in_specs=in_specs, out_specs=out_specs, check_vma=False)
```

```python
import functools
import math
import jax
import jax.numpy as jnp
import numpy as np
from jax import lax
from jax.experimental import pallas as pl
from jax.experimental.pallas import tpu as pltpu
from jax.sharding import Mesh
from jax.sharding import PartitionSpec as P

F32 = jnp.float32
BF16 = jnp.bfloat16
WIRES = (F32, F32, F32)
PINNED = 0
NT = (((1,), (1,)), ((), ()))
NN = (((1,), (0,)), ((), ()))
DEG_OF = [0] + [1] * 3 + [2] * 5 + [3] * 7 + [4] * 9
PACK_ROWS = 144
PAY_ROWS = 384


def dot(a, b, dims=NN):
    return lax.dot_general(a, b, dims, preferred_element_type=F32)


def harmonics(along_x, along_y, along_z):
    sq_x = along_x * along_x
    sq_y = along_y * along_y
    sq_z = along_z * along_z
    root3 = math.sqrt(3.0)
    root15 = math.sqrt(15.0)
    root5 = math.sqrt(5.0)
    coef_a1 = math.sqrt(35.0 / 8.0)
    coef_a2 = math.sqrt(105.0)
    coef_a3 = math.sqrt(21.0 / 8.0)
    coef_a4 = math.sqrt(7.0) / 2.0
    coef_b1 = 3.0 * math.sqrt(35.0) / 2.0
    coef_b2 = 3.0 * math.sqrt(70.0) / 4.0
    coef_b3 = 3.0 * math.sqrt(5.0) / 2.0
    coef_b4 = 3.0 * math.sqrt(10.0) / 4.0
    return [
        jnp.ones_like(along_x),
        root3 * along_y,
        root3 * along_z,
        root3 * along_x,
        root15 * along_x * along_y,
        root15 * along_y * along_z,
        root5 / 2.0 * (3.0 * sq_z - 1.0),
        root15 * along_x * along_z,
        root15 / 2.0 * (sq_x - sq_y),
        coef_a1 * along_y * (3.0 * sq_x - sq_y),
        coef_a2 * along_x * along_y * along_z,
        coef_a3 * along_y * (5.0 * sq_z - 1.0),
        coef_a4 * along_z * (5.0 * sq_z - 3.0),
        coef_a3 * along_x * (5.0 * sq_z - 1.0),
        coef_a2 / 2.0 * along_z * (sq_x - sq_y),
        coef_a1 * along_x * (sq_x - 3.0 * sq_y),
        coef_b1 * along_x * along_y * (sq_x - sq_y),
        coef_b2 * along_y * along_z * (3.0 * sq_x - sq_y),
        coef_b3 * along_x * along_y * (7.0 * sq_z - 1.0),
        coef_b4 * along_y * along_z * (7.0 * sq_z - 3.0),
        0.375 * (35.0 * sq_z * sq_z - 30.0 * sq_z + 3.0),
        coef_b4 * along_x * along_z * (7.0 * sq_z - 3.0),
        coef_b3 / 2.0 * (sq_x - sq_y) * (7.0 * sq_z - 1.0),
        coef_b2 * along_x * along_z * (sq_x - 3.0 * sq_y),
        coef_b1 / 4.0 * (sq_x * (sq_x - 3.0 * sq_y) - sq_y * (3.0 * sq_x - sq_y)),
    ]


def iota(shape, dim):
    return lax.broadcasted_iota(jnp.int32, shape, dim)


VMEM_SPEC = pl.BlockSpec(memory_space=pltpu.VMEM)


def tables_kernel(place_ref, nb_ref, valid_ref, probe_ref, cot_ref, tab_ref, cotb_ref):
    cotb_ref[...] = jnp.broadcast_to(cot_ref[...], (128, 128)).T
    slots, probes = nb_ref.shape
    groups = probes // 8
    atoms = place_ref[2]
    idx = nb_ref[...] - place_ref[0]
    idx = jnp.where(idx < 0, idx + atoms, jnp.where(idx >= atoms, idx - atoms, idx))
    idx = idx ^ place_ref[1]
    spot = (iota((probes, 256), 1) // 32) == (iota((probes, 256), 0) & 7)

    def grouped(wide):
        return jnp.sum(jnp.where(spot, wide, 0.0).reshape(groups, 8, 256), axis=1)

    tile = jnp.where((iota((slots, 256), 1) & 31) == iota((slots, 256), 0), 1.0, 0.0).astype(BF16)

    def spread_slots(x):
        return grouped(dot(x.astype(F32).T.astype(BF16), tile))

    tab_ref[0] = 256.0 * spread_slots(idx >> 8) + spread_slots(idx & 255)
    tab_ref[1] = spread_slots(valid_ref[...]) * (1.0 / math.sqrt(slots))
    pos = jnp.concatenate([probe_ref[...].astype(F32), jnp.zeros((5, probes), F32)], axis=0).T
    for i in range(3):
        tab_ref[2 + i] = grouped(jnp.broadcast_to(pos[:, i : i + 1], (probes, 256)))


def tables(place, neighbours, valid, probe_pos, cotangent):
    groups = neighbours.shape[1] // 8
    return pl.pallas_call(
        tables_kernel,
        out_shape=(jax.ShapeDtypeStruct((5, groups, 256), F32), jax.ShapeDtypeStruct((128, 128), F32)),
        in_specs=[pl.BlockSpec(memory_space=pltpu.SMEM)] + [VMEM_SPEC] * 4,
        out_specs=[VMEM_SPEC] * 2,
        compiler_params=pltpu.CompilerParams(vmem_limit_bytes=8 << 20),
        name="tables",
    )(place, neighbours, valid, probe_pos, cotangent)


def hot_rows(row, part):
    return jnp.where((iota((256, 256), 0) + 256 * part).astype(F32) == row, 1.0, 0.0).astype(BF16)


def kernel(
    b0, b1, b2, b3, b4, b5, tab_ref, w1t_ref, w2t_ref, ro_ref, cotb_ref,
    dens_ref, gf_ref, pay_ref,
    win_ref, feat_ref, pos_ref, sph_ref, rad_ref, w2_ref, dens_s, gro_s, radial_s,
    hid_ref, slope_ref, bas_ref, gr_ref,
    *, ua, ub, uc, lock,
):
    groups = tab_ref.shape[1]

    def lanes(g):
        return pl.ds(pl.multiple_of(g * 256, 256), 256)

    for i, src in enumerate((b0, b1, b2, b3, b4, b5)):
        win_ref[:, pl.ds(128 * i, 128)] = src[...]
    for l in range(5):
        w2_ref[l] = w2t_ref[:, pl.ds(128 * l, 128)].astype(F32).T.astype(BF16)

    def gather(g, carry):
        row = tab_ref[0, pl.ds(g, 1), :]
        total = None
        for part in range(3):
            piece = dot(win_ref[:, pl.ds(256 * part, 256)], hot_rows(row, part))
            total = piece if total is None else total + piece
        feat_ref[:, lanes(g)] = total[:128].astype(BF16)
        for i in range(3):
            pos_ref[i, pl.ds(g, 1), :] = total[128 + i : 129 + i]
        return carry

    lax.fori_loop(0, groups, gather, 0, unroll=ua)

    idx = tab_ref[0]
    offset = (idx >= 256.0).astype(F32) + (idx >= 512.0).astype(F32) - 1.0
    dx = pos_ref[0] - tab_ref[2]
    dy = pos_ref[1] - tab_ref[3]
    dz = pos_ref[2] + 2.0 * offset - tab_ref[4]
    radius = jnp.sqrt(dx * dx + dy * dy + dz * dz + 0.25)
    rad_ref[...] = radius
    inv = 1.0 / radius
    for k, val in enumerate(harmonics(dx * inv, dy * inv, dz * inv)):
        top = val.astype(BF16).astype(F32)
        sph_ref[0, k] = top
        sph_ref[1, k] = val - top

    gro_s[...] = jnp.zeros_like(gro_s)

    w1 = w1t_ref[...].T
    w1_top = w1.astype(BF16).astype(F32)
    w1_cat = jnp.concatenate([w1_top, w1_top, w1 - w1_top, jnp.zeros_like(w1)], axis=1).astype(BF16)

    def network(g, carry):
        offs = rad_ref[pl.ds(g, 1), :] - 0.75 * iota((8, 256), 0).astype(F32)
        basis = jnp.exp(-2.0 * offs * offs)
        basis_top = basis.astype(BF16).astype(F32)
        basis_cat = jnp.concatenate(
            [basis_top, basis - basis_top, basis_top, jnp.zeros_like(basis)], axis=0
        ).astype(BF16)
        bas_ref[:, lanes(g)] = basis_cat
        preact = dot(w1_cat, basis_cat)
        sig = 1.0 / (1.0 + jnp.exp(-preact))
        hid_ref[:, lanes(g)] = (preact * sig).astype(BF16)
        slope_ref[:, lanes(g)] = sig * (1.0 + preact * (1.0 - sig))
        return carry

    lax.fori_loop(0, groups, network, 0, unroll=ub)

    mask = iota((8, 256), 0) == iota((8, 256), 1) // 32

    def spheres(g):
        tops, lows = [], []
        for l in range(5):
            for half, out in ((0, tops), (1, lows)):
                rows = [
                    jnp.where(mask, sph_ref[half, k, pl.ds(g, 1), :], 0.0)
                    for k in range(l * l, (l + 1) * (l + 1))
                ]
                out.append(jnp.concatenate(rows, axis=0) if len(rows) > 1 else rows[0])
        return tops, lows

    def forward(g, u, sph):
        tops, lows = sph
        fw = feat_ref[:, lanes(g)].astype(F32) * tab_ref[1, pl.ds(g, 1), :]
        hidden = hid_ref[:, lanes(g)]
        msgs = []
        for l in range(5):
            radial = dot(w2_ref[l], hidden)
            radial_s[u, l] = radial
            msgs.append((radial * fw).astype(BF16))
        moms = []
        for degs in ((0, 1), (2, 3), (4,)):
            rows = jnp.concatenate([x for l in degs for x in (tops[l], lows[l])], axis=0).astype(BF16)
            right = jnp.concatenate([msgs[l] for l in degs], axis=0) if len(degs) > 1 else msgs[degs[0]]
            out = dot(rows, right, NT)
            at = 0
            for i, l in enumerate(degs):
                size = 8 * (2 * l + 1)
                cols = slice(128 * i, 128 * i + 128)
                moms.append(out[at : at + size, cols] + out[at + size : at + 2 * size, cols])
                at += 2 * size
        return moms

    def middle(g, moms):
        cot = cotb_ref[pl.ds(pl.multiple_of(g * 8, 8), 8), :]
        dens = None
        grads = []
        for l, mom in enumerate(moms):
            ro = ro_ref[pl.ds(l, 1), :]
            parts = [mom[8 * i : 8 * i + 8] for i in range(2 * l + 1)]
            if l == 0:
                squares = parts[0]
                grads.append(cot * ro)
            else:
                squares = None
                for x in parts:
                    squares = x * x if squares is None else squares + x * x
                fac = 2.0 * cot * ro
                grads.append(jnp.concatenate([x * fac for x in parts], axis=0))
            dens = squares * ro if dens is None else dens + squares * ro
            gro_s[l] += squares * cot
        dens_s[pl.ds(pl.multiple_of(g * 8, 8), 8), :] = dens
        return grads

    def backward(g, u, sph, grads):
        tops, lows = sph
        wgt = tab_ref[1, pl.ds(g, 1), :]
        fw = feat_ref[:, lanes(g)].astype(F32) * wgt
        gf = None
        for l in range(5):
            top = grads[l].astype(BF16).astype(F32)
            left = jnp.concatenate([top, top, grads[l] - top], axis=0).T.astype(BF16)
            right = jnp.concatenate([tops[l], lows[l], tops[l]], axis=0).astype(BF16)
            gmsg = dot(left, right)
            piece = gmsg * radial_s[u, l]
            gf = piece if gf is None else gf + piece
            gr_ref[pl.ds(128 * l, 128), lanes(g)] = (gmsg * fw).astype(BF16)
        gf_ref[:, lanes(g)] = (gf * wgt).astype(BF16)

    def block(i, carry):
        gs = [i * lock + u for u in range(lock)]
        sphs = [spheres(g) for g in gs]
        moms = [forward(g, u, sphs[u]) for u, g in enumerate(gs)]
        grads = [middle(g, moms[u]) for u, g in enumerate(gs)]
        for u, g in enumerate(gs):
            backward(g, u, sphs[u], grads[u])
        return carry

    lax.fori_loop(0, groups // lock, block, 0, unroll=uc)

    hid = hid_ref[...]
    gr = gr_ref[...]
    for l in range(5):
        pay_ref[pl.ds(64 * l, 64), :] = dot(hid, gr_ref[pl.ds(128 * l, 128), :], NT).astype(pay_ref.dtype)
    gpre = (dot(w2t_ref[...], gr) * slope_ref[...]).astype(BF16)
    gw1 = dot(bas_ref[...], gpre, NT)
    gw1 = gw1[:8, :] + gw1[8:16, :]
    gw1 = jnp.concatenate([gw1, jnp.zeros((8, 64), F32)], axis=1)
    gro = jnp.concatenate(
        [jnp.sum(gro_s[l], axis=0, keepdims=True) for l in range(5)] + [jnp.zeros((3, 128), F32)], axis=0
    )
    pay_ref[pl.ds(320, 16), :] = jnp.concatenate([gro, gw1], axis=0).astype(pay_ref.dtype)
    pay_ref[pl.ds(336, 48), :] = jnp.zeros((48, 128), pay_ref.dtype)
    dens_ref[...] = lax.dot_general(
        jnp.ones((8, 128), F32), dens_s[...], NT, precision=lax.Precision.HIGHEST, preferred_element_type=F32
    )


def scatter_kernel(gf_ref, tab_ref, *outs):
    groups = tab_ref.shape[1]
    for part in range(3):
        total = None
        for g in range(groups):
            row = tab_ref[0, pl.ds(g, 1), :]
            piece = dot(gf_ref[:, pl.ds(256 * g, 256)], hot_rows(row, part), NT)
            total = piece if total is None else total + piece
        total = total.astype(BF16)
        outs[part][:128] = total[:, :128]
        outs[part][128:] = total[:, 128:]


def scatter(gf, tab):
    return pl.pallas_call(
        scatter_kernel,
        out_shape=(jax.ShapeDtypeStruct((256, 128), BF16),) * 3,
        in_specs=[VMEM_SPEC] * 2,
        out_specs=[VMEM_SPEC] * 3,
        compiler_params=pltpu.CompilerParams(vmem_limit_bytes=16 << 20),
        name="scatter_feat",
    )(gf, tab)


def layer(blocks, tab, w1t, w2t, ro, cot, ua=16, ub=16, uc=1, lock=4):
    groups = tab.shape[1]
    edges = groups * 256
    return pl.pallas_call(
        functools.partial(kernel, ua=ua, ub=ub, uc=uc, lock=lock),
        out_shape=(
            jax.ShapeDtypeStruct((8, 128), F32),
            jax.ShapeDtypeStruct((128, edges), BF16),
            jax.ShapeDtypeStruct((PAY_ROWS, 128), WIRES[0]),
        ),
        in_specs=[VMEM_SPEC] * 11,
        out_specs=[VMEM_SPEC] * 3,
        scratch_shapes=[
            pltpu.VMEM((PACK_ROWS, 768), BF16),
            pltpu.VMEM((128, edges), BF16),
            pltpu.VMEM((3, groups, 256), F32),
            pltpu.VMEM((2, 25, groups, 256), F32),
            pltpu.VMEM((groups, 256), F32),
            pltpu.VMEM((5, 128, 64), BF16),
            pltpu.VMEM((128, 128), F32),
            pltpu.VMEM((5, 8, 128), F32),
            pltpu.VMEM((lock, 5, 128, 256), F32),
            pltpu.VMEM((64, edges), BF16),
            pltpu.VMEM((64, edges), F32),
            pltpu.VMEM((32, edges), BF16),
            pltpu.VMEM((640, edges), BF16),
        ],
        compiler_params=pltpu.CompilerParams(vmem_limit_bytes=32 << 20),
        name="probe_layer",
    )(*blocks, tab, w1t, w2t, ro, cot)


def finish_kernel(scale, x_ref, w1_ref, w2_ref, ro_ref):
    for l in range(5):
        w2_ref[:, pl.ds(128 * l, 128)] = x_ref[pl.ds(64 * l, 64), :] * scale
    ro_ref[...] = x_ref[pl.ds(320, 8), :][:5] * scale
    w1_ref[...] = x_ref[pl.ds(328, 8), :][:, :64] * scale


def finish(x, scale):
    return pl.pallas_call(
        functools.partial(finish_kernel, scale),
        out_shape=(
            jax.ShapeDtypeStruct((8, 64), F32),
            jax.ShapeDtypeStruct((64, 640), F32),
            jax.ShapeDtypeStruct((5, 128), F32),
        ),
        in_specs=[VMEM_SPEC],
        out_specs=[VMEM_SPEC] * 3,
        compiler_params=pltpu.CompilerParams(vmem_limit_bytes=8 << 20),
        name="finish",
    )(x)


AXES = ("z", "ylo", "x", "core", "yhi")
SLAB = ("z", "ylo", "x", "core")
NEAR = ("ylo", "x", "core")
FAR = ("z", "yhi")


def exchange(x, axes):
    return lax.all_to_all(x, axes, 0, 0, tiled=True)


def passed_along(block, distance):
    count = lax.axis_size(SLAB)
    return lax.ppermute(block, SLAB, [(i, (i + distance) % count) for i in range(count)])


def sent(block, slab_step, plane_step):
    slabs, planes = lax.axis_size(SLAB), lax.axis_size("yhi")
    route = [
        (s * planes + p, (s + slab_step) % slabs * planes + (p + plane_step) % planes)
        for s in range(slabs)
        for p in range(planes)
    ]
    return lax.ppermute(block, AXES, route)


def joined(mine, other):
    even = lax.axis_index("yhi") == 0
    return jnp.concatenate([jnp.where(even, mine, other), jnp.where(even, other, mine)], axis=1)


def totals(x, copies, wire):
    total = jnp.sum(x.astype(F32), axis=0).astype(wire)
    return jnp.broadcast_to(total[None], (copies,) + total.shape)


def shards(probe_pos, atom_pos, atom_feat, neighbours, valid, w_radial1, w_radial2, readout, cotangent):
    slab_count = lax.axis_size(SLAB)
    slab_index = lax.axis_index(SLAB)
    planes = lax.axis_size("yhi")
    plane = lax.axis_index("yhi")
    atom_dev = atom_feat.shape[1]
    atom_slab = atom_dev * planes
    pack = jnp.concatenate(
        [atom_feat, atom_pos, jnp.zeros((PACK_ROWS - 131, atom_dev), BF16)], axis=0
    )
    steps = ((-1, 0), (-1, 1), (0, 0), (0, 1), (1, 0), (1, 1))
    blocks = [pack if step == (0, 0) else sent(pack, -step[0], step[1]) for step in steps]
    place = jnp.stack(
        [(slab_index - 1) * atom_slab, plane * atom_dev, jnp.full((), slab_count * atom_slab, jnp.int32)]
    )
    tab, cot = tables(place, neighbours, valid, probe_pos, cotangent.reshape(1, -1))
    dens, edge_grad, pay = layer(
        blocks, tab, w_radial1.T, w_radial2.T, readout, cot
    )
    density = dens[0]
    near, far = lax.axis_size(NEAR), lax.axis_size(FAR)
    part = exchange(pay.reshape(near, PAY_ROWS // near, 128).astype(WIRES[0]), NEAR)
    to_low, own_grad, to_high = scatter(edge_grad, tab)
    wide = totals(part, far, WIRES[1])
    if PINNED:
        wide, to_low, to_high = lax.optimization_barrier((wide, to_low, to_high))
    part = exchange(wide, FAR)
    from_high = passed_along(to_low, -1)
    from_low = passed_along(to_high, 1)
    slab_sum = own_grad.astype(F32) + from_high.astype(F32) + from_low.astype(F32)
    wide = totals(part, near, WIRES[2])
    other = slab_sum[atom_dev:].astype(BF16)
    if PINNED > 1:
        wide, other = lax.optimization_barrier((wide, other))
    part = exchange(wide, NEAR)
    grad_feat = slab_sum[:atom_dev] + sent(other, 0, 1).astype(F32)
    scale = 1.0 / math.sqrt(neighbours.shape[1] * slab_count * planes)
    w1t, w2t, grad_ro = finish(part.reshape(PAY_ROWS, 128), scale)
    grad_w1, grad_w2 = w1t.T, w2t.T
    return density, grad_feat, grad_w1, grad_w2, grad_ro


def solution(mesh):
    fine = Mesh(np.asarray(mesh.devices).reshape(8, 2, 4, 2, 2), AXES)
    flat = P(None, AXES)
    in_specs = (flat, flat, flat, flat, flat, P(), P(), P(), P(AXES))
    out_specs = (P(AXES), flat, P(), P(), P())
    return jax.shard_map(shards, mesh=fine, in_specs=in_specs, out_specs=out_specs, check_vma=False)
```

```python
import functools
import math
import jax
import jax.numpy as jnp
import numpy as np
from jax import lax
from jax.experimental import pallas as pl
from jax.experimental.pallas import tpu as pltpu
from jax.sharding import Mesh
from jax.sharding import PartitionSpec as P

F32 = jnp.float32
BF16 = jnp.bfloat16
WIRES = (F32, F32, F32)
PINNED = 0
NT = (((1,), (1,)), ((), ()))
NN = (((1,), (0,)), ((), ()))
DEG_OF = [0] + [1] * 3 + [2] * 5 + [3] * 7 + [4] * 9
PACK_ROWS = 144
PAY_ROWS = 384


def dot(a, b, dims=NN):
    return lax.dot_general(a, b, dims, preferred_element_type=F32)


def harmonics(along_x, along_y, along_z):
    sq_x = along_x * along_x
    sq_y = along_y * along_y
    sq_z = along_z * along_z
    root3 = math.sqrt(3.0)
    root15 = math.sqrt(15.0)
    root5 = math.sqrt(5.0)
    coef_a1 = math.sqrt(35.0 / 8.0)
    coef_a2 = math.sqrt(105.0)
    coef_a3 = math.sqrt(21.0 / 8.0)
    coef_a4 = math.sqrt(7.0) / 2.0
    coef_b1 = 3.0 * math.sqrt(35.0) / 2.0
    coef_b2 = 3.0 * math.sqrt(70.0) / 4.0
    coef_b3 = 3.0 * math.sqrt(5.0) / 2.0
    coef_b4 = 3.0 * math.sqrt(10.0) / 4.0
    return [
        jnp.ones_like(along_x),
        root3 * along_y,
        root3 * along_z,
        root3 * along_x,
        root15 * along_x * along_y,
        root15 * along_y * along_z,
        root5 / 2.0 * (3.0 * sq_z - 1.0),
        root15 * along_x * along_z,
        root15 / 2.0 * (sq_x - sq_y),
        coef_a1 * along_y * (3.0 * sq_x - sq_y),
        coef_a2 * along_x * along_y * along_z,
        coef_a3 * along_y * (5.0 * sq_z - 1.0),
        coef_a4 * along_z * (5.0 * sq_z - 3.0),
        coef_a3 * along_x * (5.0 * sq_z - 1.0),
        coef_a2 / 2.0 * along_z * (sq_x - sq_y),
        coef_a1 * along_x * (sq_x - 3.0 * sq_y),
        coef_b1 * along_x * along_y * (sq_x - sq_y),
        coef_b2 * along_y * along_z * (3.0 * sq_x - sq_y),
        coef_b3 * along_x * along_y * (7.0 * sq_z - 1.0),
        coef_b4 * along_y * along_z * (7.0 * sq_z - 3.0),
        0.375 * (35.0 * sq_z * sq_z - 30.0 * sq_z + 3.0),
        coef_b4 * along_x * along_z * (7.0 * sq_z - 3.0),
        coef_b3 / 2.0 * (sq_x - sq_y) * (7.0 * sq_z - 1.0),
        coef_b2 * along_x * along_z * (sq_x - 3.0 * sq_y),
        coef_b1 / 4.0 * (sq_x * (sq_x - 3.0 * sq_y) - sq_y * (3.0 * sq_x - sq_y)),
    ]


def iota(shape, dim):
    return lax.broadcasted_iota(jnp.int32, shape, dim)


VMEM_SPEC = pl.BlockSpec(memory_space=pltpu.VMEM)


def tables_kernel(place_ref, nb_ref, valid_ref, probe_ref, cot_ref, tab_ref, cotb_ref):
    cotb_ref[...] = jnp.broadcast_to(cot_ref[...], (128, 128)).T
    slots, probes = nb_ref.shape
    groups = probes // 8
    atoms = place_ref[2]
    idx = nb_ref[...] - place_ref[0]
    idx = jnp.where(idx < 0, idx + atoms, jnp.where(idx >= atoms, idx - atoms, idx))
    idx = idx ^ place_ref[1]
    spot = (iota((probes, 256), 1) // 32) == (iota((probes, 256), 0) & 7)

    def grouped(wide):
        return jnp.sum(jnp.where(spot, wide, 0.0).reshape(groups, 8, 256), axis=1)

    tile = jnp.where((iota((slots, 256), 1) & 31) == iota((slots, 256), 0), 1.0, 0.0).astype(BF16)

    def spread_slots(x):
        return grouped(dot(x.astype(F32).T.astype(BF16), tile))

    tab_ref[0] = 256.0 * spread_slots(idx >> 8) + spread_slots(idx & 255)
    tab_ref[1] = spread_slots(valid_ref[...]) * (1.0 / math.sqrt(slots))
    pos = jnp.concatenate([probe_ref[...].astype(F32), jnp.zeros((5, probes), F32)], axis=0).T
    for i in range(3):
        tab_ref[2 + i] = grouped(jnp.broadcast_to(pos[:, i : i + 1], (probes, 256)))


def tables(place, neighbours, valid, probe_pos, cotangent):
    groups = neighbours.shape[1] // 8
    return pl.pallas_call(
        tables_kernel,
        out_shape=(jax.ShapeDtypeStruct((5, groups, 256), F32), jax.ShapeDtypeStruct((128, 128), F32)),
        in_specs=[pl.BlockSpec(memory_space=pltpu.SMEM)] + [VMEM_SPEC] * 4,
        out_specs=[VMEM_SPEC] * 2,
        compiler_params=pltpu.CompilerParams(vmem_limit_bytes=8 << 20),
        name="tables",
    )(place, neighbours, valid, probe_pos, cotangent)


def hot_rows(row, part):
    return jnp.where((iota((256, 256), 0) + 256 * part).astype(F32) == row, 1.0, 0.0).astype(BF16)


def kernel(
    b0, b1, b2, b3, b4, b5, tab_ref, w1t_ref, w2t_ref, ro_ref, cotb_ref,
    dens_ref, gf_ref, pay_ref,
    win_ref, feat_ref, pos_ref, sph_ref, rad_ref, w2_ref, dens_s, gro_s, radial_s,
    hid_ref, slope_ref, bas_ref, gr_ref,
    *, ua, ub, uc, lock,
):
    groups = tab_ref.shape[1]

    def lanes(g):
        return pl.ds(pl.multiple_of(g * 256, 256), 256)

    for i, src in enumerate((b0, b1, b2, b3, b4, b5)):
        win_ref[:, pl.ds(128 * i, 128)] = src[...]
    for l in range(5):
        w2_ref[l] = w2t_ref[:, pl.ds(128 * l, 128)].astype(F32).T.astype(BF16)

    def gather(g, carry):
        row = tab_ref[0, pl.ds(g, 1), :]
        total = None
        for part in range(3):
            piece = dot(win_ref[:, pl.ds(256 * part, 256)], hot_rows(row, part))
            total = piece if total is None else total + piece
        feat_ref[:, lanes(g)] = total[:128].astype(BF16)
        for i in range(3):
            pos_ref[i, pl.ds(g, 1), :] = total[128 + i : 129 + i]
        return carry

    lax.fori_loop(0, groups, gather, 0, unroll=ua)

    idx = tab_ref[0]
    offset = (idx >= 256.0).astype(F32) + (idx >= 512.0).astype(F32) - 1.0
    dx = pos_ref[0] - tab_ref[2]
    dy = pos_ref[1] - tab_ref[3]
    dz = pos_ref[2] + 2.0 * offset - tab_ref[4]
    radius = jnp.sqrt(dx * dx + dy * dy + dz * dz + 0.25)
    rad_ref[...] = radius
    inv = 1.0 / radius
    for k, val in enumerate(harmonics(dx * inv, dy * inv, dz * inv)):
        top = val.astype(BF16).astype(F32)
        sph_ref[0, k] = top
        sph_ref[1, k] = val - top

    gro_s[...] = jnp.zeros_like(gro_s)

    w1 = w1t_ref[...].T
    w1_top = w1.astype(BF16).astype(F32)
    w1_cat = jnp.concatenate([w1_top, w1_top, w1 - w1_top, jnp.zeros_like(w1)], axis=1).astype(BF16)

    def network(g, carry):
        offs = rad_ref[pl.ds(g, 1), :] - 0.75 * iota((8, 256), 0).astype(F32)
        basis = jnp.exp(-2.0 * offs * offs)
        basis_top = basis.astype(BF16).astype(F32)
        basis_cat = jnp.concatenate(
            [basis_top, basis - basis_top, basis_top, jnp.zeros_like(basis)], axis=0
        ).astype(BF16)
        bas_ref[:, lanes(g)] = basis_cat
        preact = dot(w1_cat, basis_cat)
        sig = 1.0 / (1.0 + jnp.exp(-preact))
        hid_ref[:, lanes(g)] = (preact * sig).astype(BF16)
        slope_ref[:, lanes(g)] = sig * (1.0 + preact * (1.0 - sig))
        return carry

    lax.fori_loop(0, groups, network, 0, unroll=ub)

    mask = iota((8, 256), 0) == iota((8, 256), 1) // 32

    def spheres(g):
        tops, lows = [], []
        for l in range(5):
            for half, out in ((0, tops), (1, lows)):
                rows = [
                    jnp.where(mask, sph_ref[half, k, pl.ds(g, 1), :], 0.0)
                    for k in range(l * l, (l + 1) * (l + 1))
                ]
                out.append(jnp.concatenate(rows, axis=0) if len(rows) > 1 else rows[0])
        return tops, lows

    def forward(g, u, sph):
        tops, lows = sph
        fw = feat_ref[:, lanes(g)].astype(F32) * tab_ref[1, pl.ds(g, 1), :]
        hidden = hid_ref[:, lanes(g)]
        msgs = []
        for l in range(5):
            radial = dot(w2_ref[l], hidden)
            radial_s[u, l] = radial
            msgs.append((radial * fw).astype(BF16))
        moms = []
        for degs in ((0, 1), (2, 3), (4,)):
            rows = jnp.concatenate([x for l in degs for x in (tops[l], lows[l])], axis=0).astype(BF16)
            right = jnp.concatenate([msgs[l] for l in degs], axis=0) if len(degs) > 1 else msgs[degs[0]]
            out = dot(rows, right, NT)
            at = 0
            for i, l in enumerate(degs):
                size = 8 * (2 * l + 1)
                cols = slice(128 * i, 128 * i + 128)
                moms.append(out[at : at + size, cols] + out[at + size : at + 2 * size, cols])
                at += 2 * size
        return moms

    def middle(g, moms):
        cot = cotb_ref[pl.ds(pl.multiple_of(g * 8, 8), 8), :]
        dens = None
        grads = []
        for l, mom in enumerate(moms):
            ro = ro_ref[pl.ds(l, 1), :]
            parts = [mom[8 * i : 8 * i + 8] for i in range(2 * l + 1)]
            if l == 0:
                squares = parts[0]
                grads.append(cot * ro)
            else:
                squares = None
                for x in parts:
                    squares = x * x if squares is None else squares + x * x
                fac = 2.0 * cot * ro
                grads.append(jnp.concatenate([x * fac for x in parts], axis=0))
            dens = squares * ro if dens is None else dens + squares * ro
            gro_s[l] += squares * cot
        dens_s[pl.ds(pl.multiple_of(g * 8, 8), 8), :] = dens
        return grads

    def backward(g, u, sph, grads):
        tops, lows = sph
        wgt = tab_ref[1, pl.ds(g, 1), :]
        fw = feat_ref[:, lanes(g)].astype(F32) * wgt
        gf = None
        for l in range(5):
            top = grads[l].astype(BF16).astype(F32)
            left = jnp.concatenate([top, top, grads[l] - top], axis=0).T.astype(BF16)
            right = jnp.concatenate([tops[l], lows[l], tops[l]], axis=0).astype(BF16)
            gmsg = dot(left, right)
            piece = gmsg * radial_s[u, l]
            gf = piece if gf is None else gf + piece
            gr_ref[pl.ds(128 * l, 128), lanes(g)] = (gmsg * fw).astype(BF16)
        gf_ref[:, lanes(g)] = (gf * wgt).astype(BF16)

    def block(i, carry):
        gs = [i * lock + u for u in range(lock)]
        sphs = [spheres(g) for g in gs]
        moms = [forward(g, u, sphs[u]) for u, g in enumerate(gs)]
        grads = [middle(g, moms[u]) for u, g in enumerate(gs)]
        for u, g in enumerate(gs):
            backward(g, u, sphs[u], grads[u])
        return carry

    lax.fori_loop(0, groups // lock, block, 0, unroll=uc)

    hid = hid_ref[...]
    gr = gr_ref[...]
    for l in range(5):
        pay_ref[pl.ds(64 * l, 64), :] = dot(hid, gr_ref[pl.ds(128 * l, 128), :], NT).astype(pay_ref.dtype)
    gpre = (dot(w2t_ref[...], gr) * slope_ref[...]).astype(BF16)
    gw1 = dot(bas_ref[...], gpre, NT)
    gw1 = gw1[:8, :] + gw1[8:16, :]
    gw1 = jnp.concatenate([gw1, jnp.zeros((8, 64), F32)], axis=1)
    gro = jnp.concatenate(
        [jnp.sum(gro_s[l], axis=0, keepdims=True) for l in range(5)] + [jnp.zeros((3, 128), F32)], axis=0
    )
    pay_ref[pl.ds(320, 16), :] = jnp.concatenate([gro, gw1], axis=0).astype(pay_ref.dtype)
    pay_ref[pl.ds(336, 48), :] = jnp.zeros((48, 128), pay_ref.dtype)
    dens_ref[...] = lax.dot_general(
        jnp.ones((8, 128), F32), dens_s[...], NT, precision=lax.Precision.HIGHEST, preferred_element_type=F32
    )


def scatter_kernel(gf_ref, tab_ref, *outs):
    groups = tab_ref.shape[1]
    for part in range(3):
        total = None
        for g in range(groups):
            row = tab_ref[0, pl.ds(g, 1), :]
            piece = dot(gf_ref[:, pl.ds(256 * g, 256)], hot_rows(row, part), NT)
            total = piece if total is None else total + piece
        total = total.astype(BF16)
        outs[part][:128] = total[:, :128]
        outs[part][128:] = total[:, 128:]


def scatter(gf, tab):
    return pl.pallas_call(
        scatter_kernel,
        out_shape=(jax.ShapeDtypeStruct((256, 128), BF16),) * 3,
        in_specs=[VMEM_SPEC] * 2,
        out_specs=[VMEM_SPEC] * 3,
        compiler_params=pltpu.CompilerParams(vmem_limit_bytes=16 << 20),
        name="scatter_feat",
    )(gf, tab)


def layer(blocks, tab, w1t, w2t, ro, cot, ua=16, ub=16, uc=2, lock=4):
    groups = tab.shape[1]
    edges = groups * 256
    return pl.pallas_call(
        functools.partial(kernel, ua=ua, ub=ub, uc=uc, lock=lock),
        out_shape=(
            jax.ShapeDtypeStruct((8, 128), F32),
            jax.ShapeDtypeStruct((128, edges), BF16),
            jax.ShapeDtypeStruct((PAY_ROWS, 128), WIRES[0]),
        ),
        in_specs=[VMEM_SPEC] * 11,
        out_specs=[VMEM_SPEC] * 3,
        scratch_shapes=[
            pltpu.VMEM((PACK_ROWS, 768), BF16),
            pltpu.VMEM((128, edges), BF16),
            pltpu.VMEM((3, groups, 256), F32),
            pltpu.VMEM((2, 25, groups, 256), F32),
            pltpu.VMEM((groups, 256), F32),
            pltpu.VMEM((5, 128, 64), BF16),
            pltpu.VMEM((128, 128), F32),
            pltpu.VMEM((5, 8, 128), F32),
            pltpu.VMEM((lock, 5, 128, 256), F32),
            pltpu.VMEM((64, edges), BF16),
            pltpu.VMEM((64, edges), F32),
            pltpu.VMEM((32, edges), BF16),
            pltpu.VMEM((640, edges), BF16),
        ],
        compiler_params=pltpu.CompilerParams(vmem_limit_bytes=32 << 20),
        name="probe_layer",
    )(*blocks, tab, w1t, w2t, ro, cot)


def finish_kernel(scale, x_ref, w1_ref, w2_ref, ro_ref):
    for l in range(5):
        w2_ref[:, pl.ds(128 * l, 128)] = x_ref[pl.ds(64 * l, 64), :] * scale
    ro_ref[...] = x_ref[pl.ds(320, 8), :][:5] * scale
    w1_ref[...] = x_ref[pl.ds(328, 8), :][:, :64] * scale


def finish(x, scale):
    return pl.pallas_call(
        functools.partial(finish_kernel, scale),
        out_shape=(
            jax.ShapeDtypeStruct((8, 64), F32),
            jax.ShapeDtypeStruct((64, 640), F32),
            jax.ShapeDtypeStruct((5, 128), F32),
        ),
        in_specs=[VMEM_SPEC],
        out_specs=[VMEM_SPEC] * 3,
        compiler_params=pltpu.CompilerParams(vmem_limit_bytes=8 << 20),
        name="finish",
    )(x)


AXES = ("z", "ylo", "x", "core", "yhi")
SLAB = ("z", "ylo", "x", "core")
NEAR = ("ylo", "x", "core")
FAR = ("z", "yhi")


def exchange(x, axes):
    return lax.all_to_all(x, axes, 0, 0, tiled=True)


def passed_along(block, distance):
    count = lax.axis_size(SLAB)
    return lax.ppermute(block, SLAB, [(i, (i + distance) % count) for i in range(count)])


def sent(block, slab_step, plane_step):
    slabs, planes = lax.axis_size(SLAB), lax.axis_size("yhi")
    route = [
        (s * planes + p, (s + slab_step) % slabs * planes + (p + plane_step) % planes)
        for s in range(slabs)
        for p in range(planes)
    ]
    return lax.ppermute(block, AXES, route)


def joined(mine, other):
    even = lax.axis_index("yhi") == 0
    return jnp.concatenate([jnp.where(even, mine, other), jnp.where(even, other, mine)], axis=1)


def totals(x, copies, wire):
    total = jnp.sum(x.astype(F32), axis=0).astype(wire)
    return jnp.broadcast_to(total[None], (copies,) + total.shape)


def shards(probe_pos, atom_pos, atom_feat, neighbours, valid, w_radial1, w_radial2, readout, cotangent):
    slab_count = lax.axis_size(SLAB)
    slab_index = lax.axis_index(SLAB)
    planes = lax.axis_size("yhi")
    plane = lax.axis_index("yhi")
    atom_dev = atom_feat.shape[1]
    atom_slab = atom_dev * planes
    pack = jnp.concatenate(
        [atom_feat, atom_pos, jnp.zeros((PACK_ROWS - 131, atom_dev), BF16)], axis=0
    )
    steps = ((-1, 0), (-1, 1), (0, 0), (0, 1), (1, 0), (1, 1))
    blocks = [pack if step == (0, 0) else sent(pack, -step[0], step[1]) for step in steps]
    place = jnp.stack(
        [(slab_index - 1) * atom_slab, plane * atom_dev, jnp.full((), slab_count * atom_slab, jnp.int32)]
    )
    tab, cot = tables(place, neighbours, valid, probe_pos, cotangent.reshape(1, -1))
    dens, edge_grad, pay = layer(
        blocks, tab, w_radial1.T, w_radial2.T, readout, cot
    )
    density = dens[0]
    near, far = lax.axis_size(NEAR), lax.axis_size(FAR)
    part = exchange(pay.reshape(near, PAY_ROWS // near, 128).astype(WIRES[0]), NEAR)
    to_low, own_grad, to_high = scatter(edge_grad, tab)
    wide = totals(part, far, WIRES[1])
    if PINNED:
        wide, to_low, to_high = lax.optimization_barrier((wide, to_low, to_high))
    part = exchange(wide, FAR)
    from_high = passed_along(to_low, -1)
    from_low = passed_along(to_high, 1)
    slab_sum = own_grad.astype(F32) + from_high.astype(F32) + from_low.astype(F32)
    wide = totals(part, near, WIRES[2])
    other = slab_sum[atom_dev:].astype(BF16)
    if PINNED > 1:
        wide, other = lax.optimization_barrier((wide, other))
    part = exchange(wide, NEAR)
    grad_feat = slab_sum[:atom_dev] + sent(other, 0, 1).astype(F32)
    scale = 1.0 / math.sqrt(neighbours.shape[1] * slab_count * planes)
    w1t, w2t, grad_ro = finish(part.reshape(PAY_ROWS, 128), scale)
    grad_w1, grad_w2 = w1t.T, w2t.T
    return density, grad_feat, grad_w1, grad_w2, grad_ro


def solution(mesh):
    fine = Mesh(np.asarray(mesh.devices).reshape(8, 2, 4, 2, 2), AXES)
    flat = P(None, AXES)
    in_specs = (flat, flat, flat, flat, flat, P(), P(), P(), P(AXES))
    out_specs = (P(AXES), flat, P(), P(), P())
    return jax.shard_map(shards, mesh=fine, in_specs=in_specs, out_specs=out_specs, check_vma=False)
```
